256 devices in a mesh: section: 2 (over x_lo), ctx: 128 (over z, y, x_hi, core).
Axes of the slice: x: 4 (x_hi: 2, x_lo: 2; x = x_hi * 2 + x_lo), y: 4, z: 8, core: 2. Of those that a mesh axis runs over, the one named last changes fastest.
Arguments:
- stream: bfloat16 [2, 24576, 8192], P('section', 'ctx'), may hold values from -1.5 to 1.5
- queries: bfloat16 [2, 24576, 8192], P('section', 'ctx'), may hold values from -24 to 24
- keys: bfloat16 [2, 24576, 1024], P('section', 'ctx'), may hold values from -24 to 24
- values: bfloat16 [2, 24576, 1024], P('section', 'ctx'), may hold values from -6 to 6
- segments: int32 [2, 24576], P('section', 'ctx'), may hold values from 0 to 63, never falling along the last dimension, each value on 1 to 1344 neighbouring positions
Outputs:
- next_stream: bfloat16 [2, 24576, 8192], P('section', 'ctx')
The draws below stay inside these ranges and needn't reach their ends.
Inputs may be any that keep to these rules, and one draw needn't show every extreme that they name: `segments`: along each micro-batch the numbers never fall; each document holds at most (7) * 192 tokens, and one holds exactly that many.
All inputs are finite; a program needn't handle non-finite values.
Results may differ from the reference program's by a relative error of at most 0.0095.
Values may be sent and summed in bfloat16 or wider, within the bound.
A program may use at most 128 MiB of HBM per device.

```python
import math
import jax
import jax.numpy as jnp
import numpy as np
from jax import lax

HQ = 64
KVH = 8
HD = 128
TOK_DEV = 192
WINDOW = 8
D = 8192
MICRO = 2
SEQ = 24576
DOCS = 64


def draw_queries(key, part):
    repeat = HQ // KVH
    full = jnp.clip(jax.random.normal(jax.random.fold_in(key, 1), (MICRO, SEQ, KVH, repeat, HD), jnp.float32), -6.0, 6.0)
    return full.reshape(MICRO, SEQ, HQ * HD).astype(jnp.bfloat16)


def draw_keys(key, part):
    full = jnp.clip(jax.random.normal(jax.random.fold_in(key, 2), (MICRO, SEQ, KVH, HD), jnp.float32), -6.0, 6.0)
    return full.reshape(MICRO, SEQ, KVH * HD).astype(jnp.bfloat16)


def shard_levels(key, dims, split, least, largest):
    level = 1.0
    for dim, shards_of in split:
        heights = jax.random.uniform(jax.random.fold_in(jax.random.fold_in(key, 6), dim), (shards_of,), jnp.float32, least / len(split), largest / len(split))
        level = level * jnp.repeat(jnp.exp(heights), dims[dim] // shards_of).reshape((-1,) + (1,) * (len(dims) - 1 - dim))
    return level


def length_profile(count, total, most, skew):
    weights = [(1 << 20) // math.isqrt(grade ** skew) + 1 for grade in range(2, count + 1)]
    spare, counts = total - most - (count - 1), [1] * (count - 1)
    while spare > 0:
        free = [i for i in range(count - 1) if counts[i] < most]
        whole, budget = sum([weights[i] for i in free]), spare
        for i in free:
            more = min(most - counts[i], max(1, budget * weights[i] // whole), spare)
            counts[i] = counts[i] + more
            spare = spare - more
    return np.array([most] + counts)


def ragged(key, count, total, bound, slope):
    if count == 2:
        one = jax.random.randint(key, (), max(1, total - bound), min(bound, total - 1) + 1)
        return jnp.stack([one, total - one])
    sizes = jnp.asarray(length_profile(count, total, bound, slope), jnp.int32)
    pairs = (count - 1) // 2
    giver, receiver = sizes[1:1 + 2 * pairs:2], sizes[2:2 + 2 * pairs:2]
    margin = jnp.minimum(giver - 1, bound - receiver)
    passed = jax.random.randint(jax.random.fold_in(key, 1), (pairs,), 0, 1 << 20) % (margin + 1)
    sizes = sizes.at[1:1 + 2 * pairs:2].set(giver - passed).at[2:2 + 2 * pairs:2].set(receiver + passed)
    return sizes[jax.random.permutation(jax.random.fold_in(key, 2), count)]


def bell_draw(rng, extent, width, reach, pieces=(), held_as=jnp.bfloat16):
    drawn = width * jax.random.normal(rng, extent, jnp.float32)
    if pieces:
        drawn = drawn * shard_levels(rng, extent, pieces, -0.22, 0.18)
    return jnp.clip(drawn, -reach, reach).astype(held_as)


def setup_inputs(seed: int = 0) -> dict:
    key_of = jax.random.split(jax.random.key(seed), 6)
    return {
        "stream": bell_draw(key_of[0], (MICRO, SEQ, D), 0.25, 1.5, ((0, 2), (1, 128))),
        "queries": draw_queries(jax.random.fold_in(key_of[5], 71), 0),
        "keys": draw_keys(jax.random.fold_in(key_of[5], 71), 0),
        "values": bell_draw(key_of[3], (MICRO, SEQ, KVH * HD), 1.0, 6.0, ((0, 2), (1, 128))),
        "segments": jax.vmap(lambda own: jnp.searchsorted(jnp.cumsum(ragged(own, DOCS, SEQ, (WINDOW - 1) * TOK_DEV, 2)), jnp.arange(SEQ), side="right"))(jax.random.split(key_of[4], MICRO)).reshape((MICRO, SEQ)).astype(jnp.int32),
    }


def attend_block(query_rows, key_rows, value_rows, seg_query, seg_key, pos_query, pos_key):
    tok_count = query_rows.shape[0]
    key_count = key_rows.shape[0]
    repeat = HQ // KVH
    q_four = query_rows.astype(jnp.float32).reshape(tok_count, KVH, repeat, HD)
    k_three = key_rows.astype(jnp.float32).reshape(key_count, KVH, HD)
    v_three = value_rows.astype(jnp.float32).reshape(key_count, KVH, HD)
    scores = jnp.einsum("tgrd,wgd->grtw", q_four, k_three) * (HD ** -0.5)
    visible = (seg_query[:, None] == seg_key[None, :]) & (pos_key[None, :] <= pos_query[:, None])
    scores = jnp.where(visible, scores, jnp.float32(-1e30))
    top_score = jnp.max(scores, axis=-1, keepdims=True)
    expo = jnp.exp(scores - top_score)
    probs = (expo / jnp.sum(expo, axis=-1, keepdims=True)).astype(jnp.bfloat16)
    result = jnp.einsum("grtw,wgd->tgrd", probs.astype(jnp.float32), v_three)
    return result.reshape(tok_count, HQ * HD)


def reference(stream, queries, keys, values, segments):
    pad_len = (WINDOW - 1) * TOK_DEV
    win_len = WINDOW * TOK_DEV
    attended_all = []
    for micro in range(MICRO):
        key_pad = jnp.concatenate([jnp.zeros((pad_len, keys.shape[2]), keys.dtype), keys[micro]], axis=0)
        value_pad = jnp.concatenate([jnp.zeros((pad_len, values.shape[2]), values.dtype), values[micro]], axis=0)
        seg_pad = jnp.concatenate([jnp.full((pad_len,), -1, jnp.int32), segments[micro].astype(jnp.int32)], axis=0)
        query_all = queries[micro]
        seg_all = segments[micro].astype(jnp.int32)

        def one_block(block_id):
            start = (block_id * TOK_DEV).astype(jnp.int32)
            query_rows = lax.dynamic_slice_in_dim(query_all, start, TOK_DEV, 0)
            seg_query = lax.dynamic_slice_in_dim(seg_all, start, TOK_DEV, 0)
            key_rows = lax.dynamic_slice_in_dim(key_pad, start, win_len, 0)
            value_rows = lax.dynamic_slice_in_dim(value_pad, start, win_len, 0)
            seg_key = lax.dynamic_slice_in_dim(seg_pad, start, win_len, 0)
            pos_query = start + jnp.arange(TOK_DEV, dtype=jnp.int32)
            pos_key = start - pad_len + jnp.arange(win_len, dtype=jnp.int32)
            return attend_block(query_rows, key_rows, value_rows, seg_query, seg_key, pos_query, pos_key)

        blocks_out = lax.map(one_block, jnp.arange(SEQ // TOK_DEV, dtype=jnp.int32))
        attended_all.append(blocks_out.reshape(SEQ, HQ * HD))
    results = []
    for micro in range(MICRO):
        source = (micro - 1) % MICRO
        results.append((stream[source].astype(jnp.float32) + attended_all[source]).astype(jnp.bfloat16))
    return jnp.stack(results, axis=0)
```

```python
import functools

import jax
import jax.numpy as jnp
from jax import lax
from jax.experimental import pallas as pl
from jax.experimental.pallas import tpu as pltpu
from jax.sharding import PartitionSpec as P

MESH = pl.DeviceIdType.MESH
HD = 128
REPEAT = 8
TOK = 192
GROUPS = 4
PIECES = 4
HEADS = REPEAT // PIECES
SEG_ROWS = 16
SLOTS = 9
SCALE = HD ** -0.5 * 1.4426950408889634
MASKED = -1e30


def rows_of(group):
    if group == 0:
        return pl.ds(0, SEG_ROWS + 2 * TOK)
    return pl.ds(SEG_ROWS + 2 * TOK * group, 2 * TOK)


def kernel(ctx, stream_ref, query_ref, key_ref, value_ref, seg_ref, out_ref,
           win, other, qv, sv, ov, bias, loc_sem, kv_send, kv_recv, qs_send, qs_recv, out_send, out_recv):
    s = lax.axis_index("section")
    c = lax.axis_index("ctx")
    k = lax.rem(c, 2)
    h = lax.rem(c // 2, 2)
    cross = 1 - 2 * k
    mate = (s, c + cross)

    def at(offset):
        return (s, lax.rem(c + offset + ctx, ctx))

    x_off = 2 - 4 * h
    barrier = pltpu.get_barrier_semaphore()
    greeted = [mate, at(x_off), at(x_off + cross), (1 - s, c), (1 - s, c + cross)]
    for hop in (4, 8, -4, -8):
        greeted += [at(hop), at(hop + cross)]
    for device in greeted:
        pl.semaphore_signal(barrier, inc=1, device_id=device, device_id_type=MESH)

    def local_kv(g):
        out = []
        for half, (buf, base) in enumerate(((win.at[7 + k], 4 * k), (other, 4 - 4 * k))):
            cols = pl.ds(pl.multiple_of((base + g) * HD, HD), HD)
            for i, ref in enumerate((key_ref, value_ref)):
                rows = pl.ds(SEG_ROWS + 2 * TOK * g + TOK * i, TOK)
                out.append(pltpu.make_async_copy(ref.at[0, :, cols], buf.at[rows], loc_sem.at[2 * half + i, g]))
        return out

    def local_qs(g):
        cols = pl.ds(pl.multiple_of((4 * k + g) * REPEAT * HD, REPEAT * HD), REPEAT * HD)
        return [
            pltpu.make_async_copy(query_ref.at[0, :, cols], qv.at[k, g], loc_sem.at[4, g]),
            pltpu.make_async_copy(stream_ref.at[0, :, cols], sv.at[k, g], loc_sem.at[5, g]),
        ]

    def mate_qs(g):
        cols = pl.ds(pl.multiple_of((4 - 4 * k + g) * REPEAT * HD, REPEAT * HD), REPEAT * HD)
        return [
            pltpu.make_async_remote_copy(
                src_ref=ref.at[0, :, cols], dst_ref=buf.at[k, g], send_sem=qs_send.at[i, g], recv_sem=qs_recv.at[i, g],
                device_id=mate, device_id_type=MESH)
            for i, (ref, buf) in enumerate(((query_ref, qv), (stream_ref, sv)))
        ]

    def kv_copy(src, slot, g, device, sem):
        return pltpu.make_async_remote_copy(
            src_ref=src.at[rows_of(g)], dst_ref=win.at[slot].at[rows_of(g)],
            send_sem=kv_send.at[sem, g], recv_sem=kv_recv.at[slot, g], device_id=device, device_id_type=MESH)

    def arrived(slot, g):
        kv_copy(win.at[slot], slot, g, mate, 0).wait_recv()

    own = win.at[7 + k]

    def sends(g):
        near = [kv_copy(other, 7 + k, g, mate, 0),
                kv_copy(own, 3 + k, g, at(4), 1), kv_copy(other, 3 + k, g, at(4 + cross), 2)]
        far = [kv_copy(own, 0, g, at(8), 3), kv_copy(other, 0, g, at(8 + cross), 4)]
        across = [kv_copy(own, 5 + k, g, at(2), 5), kv_copy(other, 5 + k, g, at(2 + cross), 6)]
        onward = [kv_copy(win.at[3], 5, g, at(-2), 5), kv_copy(win.at[4], 6, g, at(-2), 6)]
        forward = [kv_copy(win.at[5], 1, g, at(4), 7), kv_copy(win.at[6], 2, g, at(4), 8)]
        return near, far, across, onward, forward

    def start(copies):
        for copy in copies:
            copy.start()

    def own_send(g):
        near, far, across, _, _ = sends(g)
        for copy in local_kv(g):
            copy.wait()

        @pl.when(h == 0)
        def _():
            start(across)
        start(near)

        @pl.when(k == 1)
        def _():
            start(far)

    def pass_on(g):
        _, _, _, onward, forward = sends(g)

        @pl.when(h == 1)
        def _():
            for i in range(2):
                arrived(3 + i, g)
                onward[i].start()
        for i in range(2):
            arrived(5 + i, g)
            forward[i].start()

    def rest(g):
        @pl.when(h == 0)
        def _():
            arrived(3, g)
            arrived(4, g)
        arrived(8 - k, g)
        for slot in range(3):
            arrived(slot, g)
        for copy in local_qs(g):
            copy.wait()
        for copy in mate_qs(g):
            copy.wait_recv()

    start(local_kv(0))
    for g in range(GROUPS):
        if g:
            start(local_kv(g))
        start(local_qs(g))

    lane = lax.broadcasted_iota(jnp.int32, (16, 128), 1)
    row = lax.broadcasted_iota(jnp.int32, (16, 128), 0)
    seg = seg_ref[...].astype(jnp.float32)
    first = jnp.broadcast_to(seg[:, :128], (16, 128))
    last = jnp.broadcast_to(jnp.concatenate([seg[:, 128:], jnp.zeros((1, 64), jnp.float32)], axis=1), (16, 128))
    first_moved = pltpu.roll(first, 64, 1)
    last_moved = pltpu.roll(last, 64, 1)
    tile = jnp.where(row == 0, first, jnp.where(row == 1, last, jnp.where(
        row == 2, jnp.where(lane >= 64, first_moved, 0.0), jnp.where(lane < 64, first_moved, last_moved))))
    tile = tile.astype(jnp.bfloat16)
    win[7 + k, pl.ds(0, 16), :] = tile
    other[pl.ds(0, 16), :] = tile

    pl.semaphore_wait(barrier, len(greeted))

    own_send(0)
    for g in range(GROUPS):
        start(mate_qs(g))
    pass_on(0)
    own_send(1)
    rest(0)

    q_row = lax.broadcasted_iota(jnp.int32, (TOK, 128), 0)
    k_lane = lax.broadcasted_iota(jnp.int32, (TOK, 128), 1)
    seg_rows = [win[w, pl.ds(0, 16), :].astype(jnp.float32) for w in range(SLOTS)]
    for j in range(2):
        mine = seg_rows[7 + j]
        column = jnp.sum(
            jnp.where(q_row == k_lane, mine[0:1], 0.0) + jnp.where(q_row == k_lane + 128, mine[1:2], 0.0),
            axis=1, keepdims=True)
        begin = (c - k - 7 + j) * TOK
        for m in range(12):
            a, b = seg_rows[j + 2 * (m // 3)], seg_rows[j + 2 * (m // 3) + 1]
            keys_seg = (a[0:1], a[1:2] + b[2:3], b[3:4])[m % 3]
            seen = (column == keys_seg) & (k_lane + 128 * m <= q_row + 7 * TOK) & (k_lane + 128 * m + begin >= 0)
            bias[j, :, 128 * m:128 * (m + 1)] = jnp.where(seen, 0.0, MASKED)

    def out_copy(j, g, piece, sem):
        cols = pl.ds(pl.multiple_of((4 * k + g) * REPEAT * HD + piece * HEADS * HD, HEADS * HD), HEADS * HD)
        return pltpu.make_async_remote_copy(
            src_ref=ov.at[j, g, piece], dst_ref=out_ref.at[0, :, cols],
            send_sem=out_send.at[sem], recv_sem=out_recv.at[k * GROUPS * PIECES + g * PIECES + piece],
            device_id=(1 - s, c - k + j), device_id_type=MESH)

    def step(t, _):
        g = t // (2 * PIECES)
        j = lax.rem(t // PIECES, 2)
        piece = lax.rem(t, PIECES)
        for i in range(1, GROUPS):
            @pl.when(t == 2 * PIECES * i)
            def _():
                rest(i)

            @pl.when(t == 2 * PIECES * (i - 1) + PIECES)
            def _():
                pass_on(i)
                if i + 1 < GROUPS:
                    own_send(i + 1)

        cols = pl.ds(pl.multiple_of(piece * HEADS * HD, HEADS * HD), HEADS * HD)
        q_two = qv[j, g, :, cols]
        q_rows = jnp.concatenate([q_two[:, i * HD:(i + 1) * HD] for i in range(HEADS)], axis=0)
        at_row = pl.multiple_of(SEG_ROWS + 2 * TOK * g, 16)
        key_rows = win[pl.ds(j, 8), pl.ds(at_row, TOK), :].reshape(8 * TOK, HD)
        value_rows = win[pl.ds(j, 8), pl.ds(pl.multiple_of(at_row + TOK, 16), TOK), :].reshape(8 * TOK, HD)
        score = lax.dot_general(q_rows, key_rows, (((1,), (1,)), ((), ())), preferred_element_type=jnp.float32)
        score = score.reshape(HEADS, TOK, 8 * TOK) + bias[j][None]
        top = jnp.max(score, axis=-1, keepdims=True)
        expo = jnp.exp2((score - top) * SCALE)
        total = jnp.sum(expo, axis=-1, keepdims=True)
        result = jnp.dot(expo.astype(jnp.bfloat16).reshape(HEADS * TOK, 8 * TOK), value_rows,
                         preferred_element_type=jnp.float32)
        result = result.reshape(HEADS, TOK, HD) / total
        before = sv[j, g, :, cols].astype(jnp.float32)
        for i in range(HEADS):
            ov[j, g, piece, :, i * HD:(i + 1) * HD] = (before[:, i * HD:(i + 1) * HD] + result[i]).astype(jnp.bfloat16)
        out_copy(j, g, piece, t).start()
        return 0

    lax.fori_loop(0, 2 * GROUPS * PIECES, step, 0)

    for g in range(GROUPS):
        near, far, across, onward, forward = sends(g)
        for copy in near + across + forward + mate_qs(g):
            copy.wait_send()

        @pl.when(k == 1)
        def _():
            for copy in far:
                copy.wait_send()

    def finish(t, _):
        out_copy(0, 0, 0, t).wait_send()
        pltpu.make_async_remote_copy(
            src_ref=ov.at[0, 0, 0], dst_ref=out_ref.at[0, :, pl.ds(0, HEADS * HD)],
            send_sem=out_send.at[t], recv_sem=out_recv.at[t], device_id=mate, device_id_type=MESH).wait_recv()
        return 0

    lax.fori_loop(0, 2 * GROUPS * PIECES, finish, 0)


def solution(mesh):
    ctx = mesh.shape["ctx"]
    hbm = pl.BlockSpec(memory_space=pl.ANY)

    def local(stream, queries, keys, values, segments):
        copies = 2 * GROUPS * PIECES
        return pl.pallas_call(
            functools.partial(kernel, ctx),
            out_shape=jax.ShapeDtypeStruct(stream.shape, stream.dtype),
            in_specs=[hbm, hbm, hbm, hbm, pl.BlockSpec(memory_space=pltpu.VMEM)],
            out_specs=hbm,
            scratch_shapes=[
                pltpu.VMEM((SLOTS, SEG_ROWS + 2 * TOK * GROUPS, HD), jnp.bfloat16),
                pltpu.VMEM((SEG_ROWS + 2 * TOK * GROUPS, HD), jnp.bfloat16),
                pltpu.VMEM((2, GROUPS, TOK, REPEAT * HD), jnp.bfloat16),
                pltpu.VMEM((2, GROUPS, TOK, REPEAT * HD), jnp.bfloat16),
                pltpu.VMEM((2, GROUPS, PIECES, TOK, HEADS * HD), jnp.bfloat16),
                pltpu.VMEM((2, TOK, 8 * TOK), jnp.float32),
                pltpu.SemaphoreType.DMA((6, GROUPS)),
                pltpu.SemaphoreType.DMA((9, GROUPS)),
                pltpu.SemaphoreType.DMA((SLOTS, GROUPS)),
                pltpu.SemaphoreType.DMA((2, GROUPS)),
                pltpu.SemaphoreType.DMA((2, GROUPS)),
                pltpu.SemaphoreType.DMA((copies,)),
                pltpu.SemaphoreType.DMA((copies,)),
            ],
            compiler_params=pltpu.CompilerParams(
                collective_id=0, has_side_effects=True, vmem_limit_bytes=56 << 20),
        )(stream, queries, keys, values, segments)

    spec = P("section", "ctx", None)
    return jax.shard_map(
        local, mesh=mesh, in_specs=(spec, spec, spec, spec, P("section", "ctx")), out_specs=spec, check_vma=False)
```

```python
import functools

import jax
import jax.numpy as jnp
from jax import lax
from jax.experimental import pallas as pl
from jax.experimental.pallas import tpu as pltpu
from jax.sharding import PartitionSpec as P

MESH = pl.DeviceIdType.MESH
HD = 128
REPEAT = 8
TOK = 192
GROUPS = 4
PIECES = 4
HEADS = REPEAT // PIECES
SEG_ROWS = 16
SLOTS = 11
SCALE = HD ** -0.5 * 1.4426950408889634
MASKED = -1e30


def rows_of(group):
    if group == 0:
        return pl.ds(0, SEG_ROWS + 2 * TOK)
    return pl.ds(SEG_ROWS + 2 * TOK * group, 2 * TOK)


def kernel(ctx, stream_ref, query_ref, key_ref, value_ref, seg_ref, out_ref,
           win, other, qv, sv, ov, bias, loc_sem, kv_send, kv_recv, qs_send, qs_recv, out_send, out_recv, ready, seg_own, seg_sem):
    s = lax.axis_index("section")
    c = lax.axis_index("ctx")
    k = lax.rem(c, 2)
    h = lax.rem(c // 2, 2)
    line = c // 4
    lines = ctx // 4
    cross = 1 - 2 * k
    x_off = 2 - 4 * h
    next1, next2 = line + 1 < lines, line + 2 < lines
    past1, past2 = line >= 1, line >= 2
    left = (h == 1) | past1
    left3 = jnp.where(h == 1, past1, past2)
    mate = (s, c + cross)

    def at(offset):
        return (s, lax.rem(c + offset + ctx, ctx))

    def tell(sem, device):
        pl.semaphore_signal(sem, inc=1, device_id=device, device_id_type=MESH)

    barrier = pltpu.get_barrier_semaphore()
    for device in (mate, at(x_off), at(x_off + cross), (1 - s, c), (1 - s, c + cross)):
        tell(barrier, device)

    @pl.when(next1)
    def _():
        tell(barrier, at(4))
        tell(barrier, at(4 + cross))

    @pl.when(next2 & (k == 1))
    def _():
        tell(barrier, at(8))
        tell(barrier, at(8 + cross))

    def local_kv(g):
        out = []
        for half, (buf, base) in enumerate(((win.at[7 + k], 4 * k), (other, 4 - 4 * k))):
            cols = pl.ds(pl.multiple_of((base + g) * HD, HD), HD)
            for i, ref in enumerate((key_ref, value_ref)):
                rows = pl.ds(SEG_ROWS + 2 * TOK * g + TOK * i, TOK)
                out.append(pltpu.make_async_copy(ref.at[0, :, cols], buf.at[rows], loc_sem.at[2 * half + i, g]))
        return out

    def local_qs(g):
        cols = pl.ds(pl.multiple_of((4 * k + g) * REPEAT * HD, REPEAT * HD), REPEAT * HD)
        return [
            pltpu.make_async_copy(query_ref.at[0, :, cols], qv.at[k, g], loc_sem.at[4, g]),
            pltpu.make_async_copy(stream_ref.at[0, :, cols], sv.at[k, g], loc_sem.at[5, g]),
        ]

    def mate_qs(g):
        cols = pl.ds(pl.multiple_of((4 - 4 * k + g) * REPEAT * HD, REPEAT * HD), REPEAT * HD)
        return [
            pltpu.make_async_remote_copy(
                src_ref=ref.at[0, :, cols], dst_ref=buf.at[k, g], send_sem=qs_send.at[i, g], recv_sem=qs_recv.at[i, g],
                device_id=mate, device_id_type=MESH)
            for i, (ref, buf) in enumerate(((query_ref, qv), (stream_ref, sv)))
        ]

    def kv_copy(src, slot, g, device, sem):
        return pltpu.make_async_remote_copy(
            src_ref=src.at[rows_of(g)], dst_ref=win.at[slot].at[rows_of(g)],
            send_sem=kv_send.at[sem, g], recv_sem=kv_recv.at[slot, g], device_id=device, device_id_type=MESH)

    def arrived(slot, g):
        kv_copy(win.at[slot], slot, g, mate, 0).wait_recv()

    own = win.at[7 + k]

    def to_mate(g):
        return [kv_copy(other, 7 + k, g, mate, 0)]

    def to_next1(g):
        return [kv_copy(own, 3 + k, g, at(4), 1), kv_copy(other, 3 + k, g, at(4 + cross), 2)]

    def to_next2(g):
        return [kv_copy(own, 0, g, at(8), 3), kv_copy(other, 0, g, at(8 + cross), 4)]

    def across(g):
        slot = 5 + 4 * h + k
        return [kv_copy(own, slot, g, at(x_off), 5), kv_copy(other, slot, g, at(x_off + cross), 6)]

    def onward():
        return [kv_copy(win.at[3 + i], 5 + i, 0, at(-2), 5 + i) for i in range(2)]

    def lift(g):
        return [kv_copy(win.at[9 + i], 5 + i, g, at(4), 9 + i) for i in range(2)]

    def forward(g):
        return [kv_copy(win.at[5 + i], 1 + i, g, at(4), 7 + i) for i in range(2)]

    def start(copies):
        for copy in copies:
            copy.start()

    def rows_send(g):
        @pl.when(next1)
        def _():
            start(to_next1(g))

        @pl.when(next2 & (k == 1))
        def _():
            start(to_next2(g))

    def pass_up(g):
        @pl.when(h == 0)
        def _():
            arrived(9, g)
            arrived(10, g)

            @pl.when(next1)
            def _():
                start(lift(g))

    def pass_on(g):
        @pl.when(left)
        def _():
            arrived(5, g)
            arrived(6, g)

            @pl.when(next1)
            def _():
                start(forward(g))

    def rest_near(g):
        @pl.when(past1 & ((h == 0) | (g > 0)))
        def _():
            arrived(3, g)
            arrived(4, g)
        arrived(8 - k, g)
        for copy in local_qs(g):
            copy.wait()
        for copy in mate_qs(g):
            copy.wait_recv()

    def rest_far(g):
        @pl.when(left3)
        def _():
            arrived(1, g)
            arrived(2, g)

        @pl.when(past2)
        def _():
            arrived(0, g)

    seg_copy = pltpu.make_async_copy(seg_ref, seg_own, seg_sem)
    seg_copy.start()
    for g in range(GROUPS):
        start(local_kv(g))
        start(local_qs(g))
    seg_copy.wait()

    lane = lax.broadcasted_iota(jnp.int32, (16, 128), 1)
    row = lax.broadcasted_iota(jnp.int32, (16, 128), 0)
    seg = seg_own[...].astype(jnp.float32)
    first = jnp.broadcast_to(seg[:, :128], (16, 128))
    last = jnp.broadcast_to(jnp.concatenate([seg[:, 128:], jnp.zeros((1, 64), jnp.float32)], axis=1), (16, 128))
    first_moved = pltpu.roll(first, 64, 1)
    last_moved = pltpu.roll(last, 64, 1)
    tile = jnp.where(row == 0, first, jnp.where(row == 1, last, jnp.where(
        row == 2, jnp.where(lane >= 64, first_moved, 0.0), jnp.where(lane < 64, first_moved, last_moved))))
    tile = tile.astype(jnp.bfloat16)
    win[7 + k, pl.ds(0, 16), :] = tile
    other[pl.ds(0, 16), :] = tile

    def clear(slot, _):
        win[slot] = jnp.zeros(win.shape[1:], win.dtype)
        return 0

    lax.fori_loop(0, jnp.maximum(7 - 2 * (c // 2), 0), clear, 0)

    pl.semaphore_wait(barrier, 5 + 2 * past1.astype(jnp.int32) + past2.astype(jnp.int32))

    @pl.when(past1)
    def _():
        tell(ready.at[0], at(-4))
        tell(ready.at[0], at(-4 + cross))

    @pl.when(past2)
    def _():
        tell(ready.at[1], at(-7 - k))

    for copy in local_kv(0):
        copy.wait()

    @pl.when(h == 0)
    def _():
        start(across(0))
    start(to_mate(0))
    start(mate_qs(0))

    @pl.when(next1)
    def _():
        pl.semaphore_wait(ready.at[0], 2)
        start(to_next1(0))

    @pl.when(next2 & (k == 1))
    def _():
        pl.semaphore_wait(ready.at[1], 2)
        start(to_next2(0))

    for g in range(1, GROUPS):
        for copy in local_kv(g):
            copy.wait()

    @pl.when(h == 0)
    def _():
        for g in range(1, GROUPS):
            start(across(g))

    @pl.when(h == 1)
    def _():
        @pl.when(past1)
        def _():
            for i, copy in enumerate(onward()):
                arrived(3 + i, 0)
                copy.start()
        for g in range(1, GROUPS):
            start(across(g))
    pass_on(0)
    for g in range(1, GROUPS):
        start(to_mate(g))
        start(mate_qs(g))
    rows_send(1)
    pass_up(1)
    rest_near(0)

    q_row = lax.broadcasted_iota(jnp.int32, (TOK, 128), 0)
    k_lane = lax.broadcasted_iota(jnp.int32, (TOK, 128), 1)
    columns = []
    for j in range(2):
        mine = win[7 + j, pl.ds(0, 16), :].astype(jnp.float32)
        columns.append(jnp.sum(
            jnp.where(q_row == k_lane, mine[0:1], 0.0) + jnp.where(q_row == k_lane + 128, mine[1:2], 0.0),
            axis=1, keepdims=True))

    def mask(pairs):
        for j, pair in pairs:
            a, b = (win[j + 2 * pair + i, pl.ds(0, 16), :].astype(jnp.float32) for i in range(2))
            begin = (c - k - 7 + j) * TOK
            for i, keys_seg in enumerate((a[0:1], a[1:2] + b[2:3], b[3:4])):
                m = 3 * pair + i
                seen = (columns[j] == keys_seg) & (k_lane + 128 * m <= q_row + 7 * TOK) & (k_lane + 128 * m + begin >= 0)
                bias[j, :, 128 * m:128 * (m + 1)] = jnp.where(seen, 0.0, MASKED)

    mask(((0, 2), (0, 3), (1, 1), (1, 2), (1, 3)))
    rest_far(0)
    mask(((0, 0), (0, 1), (1, 0)))

    def out_copy(j, g, piece, sem):
        cols = pl.ds(pl.multiple_of((4 * k + g) * REPEAT * HD + piece * HEADS * HD, HEADS * HD), HEADS * HD)
        return pltpu.make_async_remote_copy(
            src_ref=ov.at[j, g, piece], dst_ref=out_ref.at[0, :, cols],
            send_sem=out_send.at[sem], recv_sem=out_recv.at[k * GROUPS * PIECES + g * PIECES + piece],
            device_id=(1 - s, c - k + j), device_id_type=MESH)

    def step(t, _):
        g = t // (2 * PIECES)
        j = lax.rem(t // PIECES, 2)
        piece = lax.rem(t, PIECES)
        for i in range(1, GROUPS):
            @pl.when(t == 2 * PIECES * i)
            def _():
                rest_near(i)
                rest_far(i)

            @pl.when(t == 2 * PIECES * (i - 1) + PIECES)
            def _():
                pass_on(i)
                if i + 1 < GROUPS:
                    rows_send(i + 1)
                    pass_up(i + 1)

        cols = pl.ds(pl.multiple_of(piece * HEADS * HD, HEADS * HD), HEADS * HD)
        q_two = qv[j, g, :, cols]
        q_rows = jnp.concatenate([q_two[:, i * HD:(i + 1) * HD] for i in range(HEADS)], axis=0)
        at_row = pl.multiple_of(SEG_ROWS + 2 * TOK * g, 16)
        key_rows = win[pl.ds(j, 8), pl.ds(at_row, TOK), :].reshape(8 * TOK, HD)
        value_rows = win[pl.ds(j, 8), pl.ds(pl.multiple_of(at_row + TOK, 16), TOK), :].reshape(8 * TOK, HD)
        score = lax.dot_general(q_rows, key_rows, (((1,), (1,)), ((), ())), preferred_element_type=jnp.float32)
        score = score.reshape(HEADS, TOK, 8 * TOK) + bias[j][None]
        top = jnp.max(score, axis=-1, keepdims=True)
        expo = jnp.exp2((score - top) * SCALE)
        total = jnp.sum(expo, axis=-1, keepdims=True)
        result = jnp.dot(expo.astype(jnp.bfloat16).reshape(HEADS * TOK, 8 * TOK), value_rows,
                         preferred_element_type=jnp.float32)
        result = result.reshape(HEADS, TOK, HD) / total
        before = sv[j, g, :, cols].astype(jnp.float32)
        for i in range(HEADS):
            ov[j, g, piece, :, i * HD:(i + 1) * HD] = (before[:, i * HD:(i + 1) * HD] + result[i]).astype(jnp.bfloat16)
        out_copy(j, g, piece, t).start()
        return 0

    lax.fori_loop(0, 2 * GROUPS * PIECES, step, 0)

    def sent(copies):
        for copy in copies:
            copy.wait_send()

    for g in range(GROUPS):
        sent(to_mate(g) + mate_qs(g))

        @pl.when((h == 0) | ((g > 0) | past1))
        def _():
            sent(across(g))

        @pl.when(next1)
        def _():
            sent(to_next1(g))
            if g:
                @pl.when(h == 0)
                def _():
                    sent(lift(g))

            @pl.when(left)
            def _():
                sent(forward(g))

        @pl.when(next2 & (k == 1))
        def _():
            sent(to_next2(g))

    def finish(t, _):
        out_copy(0, 0, 0, t).wait_send()
        pltpu.make_async_remote_copy(
            src_ref=ov.at[0, 0, 0], dst_ref=out_ref.at[0, :, pl.ds(0, HEADS * HD)],
            send_sem=out_send.at[t], recv_sem=out_recv.at[t], device_id=mate, device_id_type=MESH).wait_recv()
        return 0

    lax.fori_loop(0, 2 * GROUPS * PIECES, finish, 0)


def solution(mesh):
    ctx = mesh.shape["ctx"]
    hbm = pl.BlockSpec(memory_space=pltpu.HBM)

    def local(stream, queries, keys, values, segments):
        copies = 2 * GROUPS * PIECES
        return pl.pallas_call(
            functools.partial(kernel, ctx),
            out_shape=jax.ShapeDtypeStruct(stream.shape, stream.dtype),
            in_specs=[hbm] * 5,
            out_specs=pl.BlockSpec(memory_space=pltpu.VMEM),
            scratch_shapes=[
                pltpu.VMEM((SLOTS, SEG_ROWS + 2 * TOK * GROUPS, HD), jnp.bfloat16),
                pltpu.VMEM((SEG_ROWS + 2 * TOK * GROUPS, HD), jnp.bfloat16),
                pltpu.VMEM((2, GROUPS, TOK, REPEAT * HD), jnp.bfloat16),
                pltpu.VMEM((2, GROUPS, TOK, REPEAT * HD), jnp.bfloat16),
                pltpu.VMEM((2, GROUPS, PIECES, TOK, HEADS * HD), jnp.bfloat16),
                pltpu.VMEM((2, TOK, 8 * TOK), jnp.float32),
                pltpu.SemaphoreType.DMA((6, GROUPS)),
                pltpu.SemaphoreType.DMA((11, GROUPS)),
                pltpu.SemaphoreType.DMA((SLOTS, GROUPS)),
                pltpu.SemaphoreType.DMA((2, GROUPS)),
                pltpu.SemaphoreType.DMA((2, GROUPS)),
                pltpu.SemaphoreType.DMA((copies,)),
                pltpu.SemaphoreType.DMA((copies,)),
                pltpu.SemaphoreType.REGULAR((2,)),
                pltpu.VMEM((1, TOK), jnp.int32),
                pltpu.SemaphoreType.DMA,
            ],
            compiler_params=pltpu.CompilerParams(
                collective_id=0, has_side_effects=True, vmem_limit_bytes=40 << 20),
        )(*[pltpu.with_memory_space_constraint(a, pltpu.HBM) for a in (stream, queries, keys, values, segments)])

    spec = P("section", "ctx", None)
    return jax.shard_map(
        local, mesh=mesh, in_specs=(spec, spec, spec, spec, P("section", "ctx")), out_specs=spec, check_vma=False)
```

```python
import functools

import jax
import jax.numpy as jnp
from jax import lax
from jax.experimental import pallas as pl
from jax.experimental.pallas import tpu as pltpu
from jax.sharding import PartitionSpec as P

MESH = pl.DeviceIdType.MESH
HD = 128
REPEAT = 8
TOK = 192
GROUPS = 4
PIECES = 2
HEADS = REPEAT // PIECES
SEG_ROWS = 16
SLOTS = 11
SCALE = HD ** -0.5 * 1.4426950408889634
MASKED = -1e30


def rows_of(group):
    if group == 0:
        return pl.ds(0, SEG_ROWS + 2 * TOK)
    return pl.ds(SEG_ROWS + 2 * TOK * group, 2 * TOK)


def kernel(ctx, stream_ref, query_ref, key_ref, value_ref, seg_ref, out_ref,
           win, other, qv, sv, ov, bias, loc_sem, kv_send, kv_recv, qs_send, qs_recv, out_send, out_recv, seg_own, seg_sem):
    s = lax.axis_index("section")
    c = lax.axis_index("ctx")
    k = lax.rem(c, 2)
    h = lax.rem(c // 2, 2)
    line = c // 4
    lines = ctx // 4
    cross = 1 - 2 * k
    x_off = 2 - 4 * h
    next1, next2 = line + 1 < lines, line + 2 < lines
    past1, past2 = line >= 1, line >= 2
    left = (h == 1) | past1
    left3 = jnp.where(h == 1, past1, past2)
    mate = (s, c + cross)

    def at(offset):
        return (s, lax.rem(c + offset + ctx, ctx))

    def tell(sem, device):
        pl.semaphore_signal(sem, inc=1, device_id=device, device_id_type=MESH)

    barrier = pltpu.get_barrier_semaphore()
    for device in (mate, at(x_off), at(x_off + cross), (1 - s, c), (1 - s, c + cross)):
        tell(barrier, device)

    for there, offsets in (
        (next1, (4, 4 + cross)), (past1, (-4, -4 + cross)),
        (next2 & (k == 1), (8, 8 + cross)), (past2, (-7 - k,)),
        (next1 & (h == 1), (2, 2 + cross)), (past1 & (h == 0), (-2, -2 + cross)),
    ):
        @pl.when(there)
        def _():
            for offset in offsets:
                tell(barrier, at(offset))

    def local_kv(g):
        out = []
        for half, (buf, base) in enumerate(((win.at[7 + k], 4 * k), (other, 4 - 4 * k))):
            cols = pl.ds(pl.multiple_of((base + g) * HD, HD), HD)
            for i, ref in enumerate((key_ref, value_ref)):
                rows = pl.ds(SEG_ROWS + 2 * TOK * g + TOK * i, TOK)
                out.append(pltpu.make_async_copy(ref.at[0, :, cols], buf.at[rows], loc_sem.at[2 * half + i, g]))
        return out

    def local_qs(g):
        cols = pl.ds(pl.multiple_of((4 * k + g) * REPEAT * HD, REPEAT * HD), REPEAT * HD)
        return [
            pltpu.make_async_copy(query_ref.at[0, :, cols], qv.at[k, g], loc_sem.at[4, g]),
            pltpu.make_async_copy(stream_ref.at[0, :, cols], sv.at[k, g], loc_sem.at[5, g]),
        ]

    def mate_qs(g):
        cols = pl.ds(pl.multiple_of((4 - 4 * k + g) * REPEAT * HD, REPEAT * HD), REPEAT * HD)
        return [
            pltpu.make_async_remote_copy(
                src_ref=ref.at[0, :, cols], dst_ref=buf.at[k, g], send_sem=qs_send.at[i, g], recv_sem=qs_recv.at[i, g],
                device_id=mate, device_id_type=MESH)
            for i, (ref, buf) in enumerate(((query_ref, qv), (stream_ref, sv)))
        ]

    def kv_copy(src, slot, g, device, sem):
        return pltpu.make_async_remote_copy(
            src_ref=src.at[rows_of(g)], dst_ref=win.at[slot].at[rows_of(g)],
            send_sem=kv_send.at[sem, g], recv_sem=kv_recv.at[slot, g], device_id=device, device_id_type=MESH)

    def arrived(slot, g):
        kv_copy(win.at[slot], slot, g, mate, 0).wait_recv()

    own = win.at[7 + k]

    def to_mate(g):
        return [kv_copy(other, 7 + k, g, mate, 0)]

    def to_next1(g):
        return [kv_copy(own, 3 + k, g, at(4), 1), kv_copy(other, 3 + k, g, at(4 + cross), 2)]

    def to_next2(g):
        return [kv_copy(own, 0, g, at(8), 3), kv_copy(other, 0, g, at(8 + cross), 4)]

    def across(g):
        slot = 5 + 4 * h + k
        return [kv_copy(own, slot, g, at(x_off), 5), kv_copy(other, slot, g, at(x_off + cross), 6)]

    def to_next_first():
        return [kv_copy(own, 5 + k, 0, at(2), 5), kv_copy(other, 5 + k, 0, at(2 + cross), 6)]

    def lift(g):
        return [kv_copy(win.at[9 + i], 5 + i, g, at(4), 9 + i) for i in range(2)]

    def forward(g):
        return [kv_copy(win.at[5 + i], 1 + i, g, at(4), 7 + i) for i in range(2)]

    def start(copies):
        for copy in copies:
            copy.start()

    def rows_send(g):
        @pl.when(next1)
        def _():
            start(to_next1(g))

        @pl.when(next2 & (k == 1))
        def _():
            start(to_next2(g))

    def pass_up(g):
        @pl.when(h == 0)
        def _():
            arrived(9, g)
            arrived(10, g)

            @pl.when(next1)
            def _():
                start(lift(g))

    def pass_on(g):
        @pl.when(left)
        def _():
            arrived(5, g)
            arrived(6, g)

            @pl.when(next1)
            def _():
                start(forward(g))

    def rest_near(g):
        @pl.when(past1)
        def _():
            arrived(3, g)
            arrived(4, g)
        arrived(8 - k, g)
        for copy in local_qs(g):
            copy.wait()
        for copy in mate_qs(g):
            copy.wait_recv()

    def rest_far(g):
        @pl.when(left3)
        def _():
            arrived(1, g)
            arrived(2, g)

        @pl.when(past2)
        def _():
            arrived(0, g)

    seg_copy = pltpu.make_async_copy(seg_ref, seg_own, seg_sem)
    seg_copy.start()
    for g in range(GROUPS):
        start(local_kv(g))
        start(local_qs(g))
    seg_copy.wait()

    lane = lax.broadcasted_iota(jnp.int32, (16, 128), 1)
    row = lax.broadcasted_iota(jnp.int32, (16, 128), 0)
    seg = seg_own[...].astype(jnp.float32)
    first = jnp.broadcast_to(seg[:, :128], (16, 128))
    last = jnp.broadcast_to(jnp.concatenate([seg[:, 128:], jnp.zeros((1, 64), jnp.float32)], axis=1), (16, 128))
    first_moved = pltpu.roll(first, 64, 1)
    last_moved = pltpu.roll(last, 64, 1)
    tile = jnp.where(row == 0, first, jnp.where(row == 1, last, jnp.where(
        row == 2, jnp.where(lane >= 64, first_moved, 0.0), jnp.where(lane < 64, first_moved, last_moved))))
    tile = tile.astype(jnp.bfloat16)
    win[7 + k, pl.ds(0, 16), :] = tile
    other[pl.ds(0, 16), :] = tile

    def clear(slot, _):
        win[slot] = jnp.zeros(win.shape[1:], win.dtype)
        return 0

    lax.fori_loop(0, jnp.maximum(7 - 2 * (c // 2), 0), clear, 0)

    def count(flag, times):
        return times * flag.astype(jnp.int32)

    pl.semaphore_wait(barrier, 5 + count(next1, 2) + count(past1, 2) + count(next2 & (k == 1), 2) + count(past2, 1)
                      + count(next1 & (h == 1), 2) + count(past1 & (h == 0), 2))

    for copy in local_kv(0):
        copy.wait()

    @pl.when(h == 0)
    def _():
        start(across(0))

    @pl.when(next1 & (h == 1))
    def _():
        start(to_next_first())
    start(to_mate(0))
    start(mate_qs(0))

    @pl.when(next1)
    def _():
        start(to_next1(0))

    @pl.when(next2 & (k == 1))
    def _():
        start(to_next2(0))

    for g in range(1, GROUPS):
        for copy in local_kv(g):
            copy.wait()
        start(across(g))
    pass_on(0)
    pass_up(1)
    rows_send(1)
    for g in range(1, GROUPS):
        start(to_mate(g))
        start(mate_qs(g))
    rest_near(0)

    q_row = lax.broadcasted_iota(jnp.int32, (TOK, 128), 0)
    k_lane = lax.broadcasted_iota(jnp.int32, (TOK, 128), 1)
    columns = []
    for j in range(2):
        mine = win[7 + j, pl.ds(0, 16), :].astype(jnp.float32)
        columns.append(jnp.sum(
            jnp.where(q_row == k_lane, mine[0:1], 0.0) + jnp.where(q_row == k_lane + 128, mine[1:2], 0.0),
            axis=1, keepdims=True))

    def mask(pairs):
        for j, pair in pairs:
            a, b = (win[j + 2 * pair + i, pl.ds(0, 16), :].astype(jnp.float32) for i in range(2))
            begin = (c - k - 7 + j) * TOK
            for i, keys_seg in enumerate((a[0:1], a[1:2] + b[2:3], b[3:4])):
                m = 3 * pair + i
                seen = (columns[j] == keys_seg) & (k_lane + 128 * m <= q_row + 7 * TOK) & (k_lane + 128 * m + begin >= 0)
                bias[j, :, 128 * m:128 * (m + 1)] = jnp.where(seen, 0.0, MASKED)

    mask(((0, 2), (0, 3), (1, 1), (1, 2), (1, 3)))
    rest_far(0)
    mask(((0, 0), (0, 1), (1, 0)))

    def out_copy(j, g, piece, sem):
        cols = pl.ds(pl.multiple_of((4 * k + g) * REPEAT * HD + piece * HEADS * HD, HEADS * HD), HEADS * HD)
        return pltpu.make_async_remote_copy(
            src_ref=ov.at[j, g, piece], dst_ref=out_ref.at[0, :, cols],
            send_sem=out_send.at[sem], recv_sem=out_recv.at[k * GROUPS * PIECES + g * PIECES + piece],
            device_id=(1 - s, c - k + j), device_id_type=MESH)

    def step(t, _):
        g = t // (2 * PIECES)
        j = lax.rem(t // PIECES, 2)
        piece = lax.rem(t, PIECES)
        for i in range(1, GROUPS):
            @pl.when(t == 2 * PIECES * i)
            def _():
                rest_near(i)
                rest_far(i)

            @pl.when(t == 2 * PIECES * (i - 1) + 1)
            def _():
                pass_on(i)
                if i + 1 < GROUPS:
                    pass_up(i + 1)
                    rows_send(i + 1)

        cols = pl.ds(pl.multiple_of(piece * HEADS * HD, HEADS * HD), HEADS * HD)
        at_row = pl.multiple_of(SEG_ROWS + 2 * TOK * g, 16)
        key_rows = win[pl.ds(j, 8), pl.ds(at_row, TOK), :].reshape(8 * TOK, HD)
        value_rows = win[pl.ds(j, 8), pl.ds(pl.multiple_of(at_row + TOK, 16), TOK), :].reshape(8 * TOK, HD)
        q_all = qv[j, g, :, cols]
        before = sv[j, g, :, cols].astype(jnp.float32)

        def score_of(i):
            score = lax.dot_general(
                q_all[:, i * HD:(i + 1) * HD], key_rows, (((1,), (1,)), ((), ())), preferred_element_type=jnp.float32)
            return score + bias[j]

        score = score_of(0)
        for i in range(HEADS):
            later = score_of(i + 1) if i + 1 < HEADS else None
            top = jnp.max(score, axis=-1, keepdims=True)
            expo = jnp.exp2((score - top) * SCALE)
            total = jnp.sum(expo, axis=-1, keepdims=True)
            result = jnp.dot(expo.astype(jnp.bfloat16), value_rows, preferred_element_type=jnp.float32) / total
            ov[j, g, piece, :, i * HD:(i + 1) * HD] = (before[:, i * HD:(i + 1) * HD] + result).astype(jnp.bfloat16)
            score = later
        out_copy(j, g, piece, t).start()
        return 0

    lax.fori_loop(0, 2 * GROUPS * PIECES, step, 0)

    def sent(copies):
        for copy in copies:
            copy.wait_send()

    for g in range(GROUPS):
        sent(to_mate(g) + mate_qs(g))

        if g:
            sent(across(g))
        else:
            @pl.when((h == 0) | next1)
            def _():
                sent(across(0))

        @pl.when(next1)
        def _():
            sent(to_next1(g))
            if g:
                @pl.when(h == 0)
                def _():
                    sent(lift(g))

            @pl.when(left)
            def _():
                sent(forward(g))

        @pl.when(next2 & (k == 1))
        def _():
            sent(to_next2(g))

    def finish(t, _):
        out_copy(0, 0, 0, t).wait_send()
        pltpu.make_async_remote_copy(
            src_ref=ov.at[0, 0, 0], dst_ref=out_ref.at[0, :, pl.ds(0, HEADS * HD)],
            send_sem=out_send.at[t], recv_sem=out_recv.at[t], device_id=mate, device_id_type=MESH).wait_recv()
        return 0

    lax.fori_loop(0, 2 * GROUPS * PIECES, finish, 0)


def solution(mesh):
    ctx = mesh.shape["ctx"]
    hbm = pl.BlockSpec(memory_space=pltpu.HBM)

    def local(stream, queries, keys, values, segments):
        copies = 2 * GROUPS * PIECES
        return pl.pallas_call(
            functools.partial(kernel, ctx),
            out_shape=jax.ShapeDtypeStruct(stream.shape, stream.dtype),
            in_specs=[hbm] * 5,
            out_specs=pl.BlockSpec(memory_space=pltpu.VMEM),
            scratch_shapes=[
                pltpu.VMEM((SLOTS, SEG_ROWS + 2 * TOK * GROUPS, HD), jnp.bfloat16),
                pltpu.VMEM((SEG_ROWS + 2 * TOK * GROUPS, HD), jnp.bfloat16),
                pltpu.VMEM((2, GROUPS, TOK, REPEAT * HD), jnp.bfloat16),
                pltpu.VMEM((2, GROUPS, TOK, REPEAT * HD), jnp.bfloat16),
                pltpu.VMEM((2, GROUPS, PIECES, TOK, HEADS * HD), jnp.bfloat16),
                pltpu.VMEM((2, TOK, 8 * TOK), jnp.float32),
                pltpu.SemaphoreType.DMA((6, GROUPS)),
                pltpu.SemaphoreType.DMA((11, GROUPS)),
                pltpu.SemaphoreType.DMA((SLOTS, GROUPS)),
                pltpu.SemaphoreType.DMA((2, GROUPS)),
                pltpu.SemaphoreType.DMA((2, GROUPS)),
                pltpu.SemaphoreType.DMA((copies,)),
                pltpu.SemaphoreType.DMA((copies,)),
                pltpu.VMEM((1, TOK), jnp.int32),
                pltpu.SemaphoreType.DMA,
            ],
            compiler_params=pltpu.CompilerParams(
                collective_id=0, has_side_effects=True, vmem_limit_bytes=40 << 20),
        )(*[pltpu.with_memory_space_constraint(a, pltpu.HBM) for a in (stream, queries, keys, values, segments)])

    spec = P("section", "ctx", None)
    return jax.shard_map(
        local, mesh=mesh, in_specs=(spec, spec, spec, spec, P("section", "ctx")), out_specs=spec, check_vma=False)
```

```python
import functools

import jax
import jax.numpy as jnp
from jax import lax
from jax.experimental import pallas as pl
from jax.experimental.pallas import tpu as pltpu
from jax.sharding import PartitionSpec as P

MESH = pl.DeviceIdType.MESH
HD = 128
REPEAT = 8
TOK = 192
GROUPS = 4
PIECES = 2
HEADS = REPEAT // PIECES
PARTS = REPEAT // 2
WIDE = 2 * HD
SEG_ROWS = 16
CHUNKS = ((0, 4), (1,), (2,), (3,))
SLOTS = 11
SCALE = HD ** -0.5 * 1.4426950408889634
MASKED = -1e30


def rows_of(chunk):
    if chunk == 0:
        return pl.ds(0, SEG_ROWS + TOK)
    if chunk == GROUPS:
        return pl.ds(SEG_ROWS + TOK, TOK)
    return pl.ds(SEG_ROWS + 2 * TOK * chunk, 2 * TOK)


def kernel(ctx, stream_ref, query_ref, key_ref, value_ref, seg_ref, out_ref,
           win, other, qv, sv, ov, bias, loc_sem, kv_send, kv_recv, qs_send, qs_recv, out_send, out_recv, seg_own, seg_sem):
    s = lax.axis_index("section")
    c = lax.axis_index("ctx")
    k = lax.rem(c, 2)
    h = lax.rem(c // 2, 2)
    line = c // 4
    lines = ctx // 4
    cross = 1 - 2 * k
    x_off = 2 - 4 * h
    next1 = line + 1 < lines
    past1, past2 = line >= 1, line >= 2
    left = (h == 1) | past1
    left3 = jnp.where(h == 1, past1, past2)
    mate = (s, c + cross)

    def at(offset):
        return (s, lax.rem(c + offset + ctx, ctx))

    def tell(sem, device):
        pl.semaphore_signal(sem, inc=1, device_id=device, device_id_type=MESH)

    barrier = pltpu.get_barrier_semaphore()
    for device in (mate, at(x_off), at(x_off + cross), (1 - s, c), (1 - s, c + cross)):
        tell(barrier, device)

    for there, offsets in (
        (next1, (4, 4 + cross)), (past1, (-4, -4 + cross)),
        (next1 & (h == 1), (2, 2 + cross)), (past1 & (h == 0), (-2, -2 + cross)),
    ):
        @pl.when(there)
        def _():
            for offset in offsets:
                tell(barrier, at(offset))

    def local_kv(g):
        out = []
        for half, (buf, base) in enumerate(((win.at[7 + k], 4 * k), (other, 4 - 4 * k))):
            cols = pl.ds(pl.multiple_of((base + g) * HD, HD), HD)
            for i, ref in enumerate((key_ref, value_ref)):
                rows = pl.ds(SEG_ROWS + 2 * TOK * g + TOK * i, TOK)
                out.append(pltpu.make_async_copy(ref.at[0, :, cols], buf.at[rows], loc_sem.at[2 * half + i, g]))
        return out

    def local_qs(g):
        cols = pl.ds(pl.multiple_of((4 * k + g) * REPEAT * HD, REPEAT * HD), REPEAT * HD)
        return [
            pltpu.make_async_copy(query_ref.at[0, :, cols], qv.at[k, g], loc_sem.at[4, g]),
            pltpu.make_async_copy(stream_ref.at[0, :, cols], sv.at[k, g], loc_sem.at[5, g]),
        ]

    def mate_qs(g):
        cols = pl.ds(pl.multiple_of((4 - 4 * k + g) * REPEAT * HD, REPEAT * HD), REPEAT * HD)
        return [
            pltpu.make_async_remote_copy(
                src_ref=ref.at[0, :, cols], dst_ref=buf.at[k, g], send_sem=qs_send.at[i, g], recv_sem=qs_recv.at[i, g],
                device_id=mate, device_id_type=MESH)
            for i, (ref, buf) in enumerate(((query_ref, qv), (stream_ref, sv)))
        ]

    def kv_copy(src, slot, g, device, sem):
        return pltpu.make_async_remote_copy(
            src_ref=src.at[rows_of(g)], dst_ref=win.at[slot].at[rows_of(g)],
            send_sem=kv_send.at[sem, g], recv_sem=kv_recv.at[slot, g], device_id=device, device_id_type=MESH)

    def arrived(slot, g):
        kv_copy(win.at[slot], slot, g, mate, 0).wait_recv()

    own = win.at[7 + k]

    def to_mate(g):
        return [kv_copy(other, 7 + k, g, mate, 0)]

    def to_next1(g):
        return [kv_copy(own, 3 + k, g, at(4), 1), kv_copy(other, 3 + k, g, at(4 + cross), 2)]

    def far(n):
        return [kv_copy(win.at[4], 0, n, at(4), 3)]

    def across(g):
        slot = 5 + 4 * h + k
        return [kv_copy(own, slot, g, at(x_off), 5), kv_copy(other, slot, g, at(x_off + cross), 6)]

    def to_next_first(n):
        return [kv_copy(own, 5 + k, n, at(2), 5), kv_copy(other, 5 + k, n, at(2 + cross), 6)]

    def lift(g):
        return [kv_copy(win.at[9 + i], 5 + i, g, at(4), 9 + i) for i in range(2)]

    def forward(g):
        return [kv_copy(win.at[5 + i], 1 + i, g, at(4), 7 + i) for i in range(2)]

    def start(copies):
        for copy in copies:
            copy.start()

    def rows_send(g):
        @pl.when(next1)
        def _():
            for n in CHUNKS[g]:
                start(to_next1(n))

    def pass_up(g):
        @pl.when(h == 0)
        def _():
            arrived(9, g)
            arrived(10, g)

            @pl.when(next1)
            def _():
                start(lift(g))

    def pass_on(g):
        @pl.when(past1)
        def _():
            for n in CHUNKS[g]:
                arrived(4, n)

                @pl.when(next1)
                def _():
                    start(far(n))

        @pl.when(left)
        def _():
            for n in CHUNKS[g]:
                for i in range(2):
                    arrived(5 + i, n)

                    @pl.when(next1)
                    def _():
                        start(forward(n)[i:i + 1])

    def rest_near(g):
        for n in CHUNKS[g]:
            @pl.when(past1)
            def _():
                arrived(3, n)
            arrived(8 - k, n)
        for copy in local_qs(g):
            copy.wait()
        for copy in mate_qs(g):
            copy.wait_recv()

    def rest_far(n):
        @pl.when(left3)
        def _():
            arrived(1, n)
            arrived(2, n)

        @pl.when(past2)
        def _():
            arrived(0, n)

    seg_copy = pltpu.make_async_copy(seg_ref, seg_own, seg_sem)
    seg_copy.start()
    for g in range(GROUPS):
        start(local_kv(g))
        start(local_qs(g))
    seg_copy.wait()

    lane = lax.broadcasted_iota(jnp.int32, (16, 128), 1)
    row = lax.broadcasted_iota(jnp.int32, (16, 128), 0)
    seg = seg_own[...].astype(jnp.float32)
    first = jnp.broadcast_to(seg[:, :128], (16, 128))
    last = jnp.broadcast_to(jnp.concatenate([seg[:, 128:], jnp.zeros((1, 64), jnp.float32)], axis=1), (16, 128))
    first_moved = pltpu.roll(first, 64, 1)
    last_moved = pltpu.roll(last, 64, 1)
    tile = jnp.where(row == 0, first, jnp.where(row == 1, last, jnp.where(
        row == 2, jnp.where(lane >= 64, first_moved, 0.0), jnp.where(lane < 64, first_moved, last_moved))))
    tile = tile.astype(jnp.bfloat16)
    win[7 + k, pl.ds(0, 16), :] = tile
    other[pl.ds(0, 16), :] = tile

    def clear(slot, _):
        win[slot] = jnp.zeros(win.shape[1:], win.dtype)
        return 0

    lax.fori_loop(0, jnp.maximum(7 - 2 * (c // 2), 0), clear, 0)

    def count(flag, times):
        return times * flag.astype(jnp.int32)

    pl.semaphore_wait(barrier, 5 + count(next1, 2) + count(past1, 2)
                      + count(next1 & (h == 1), 2) + count(past1 & (h == 0), 2))

    for copy in local_kv(0):
        copy.wait()

    for n in CHUNKS[0]:
        @pl.when(h == 0)
        def _():
            start(across(n))

        @pl.when(next1 & (h == 1))
        def _():
            start(to_next_first(n))
    for n in CHUNKS[0]:
        start(to_mate(n))
    start(mate_qs(0))
    rows_send(0)

    for g in range(1, GROUPS):
        for copy in local_kv(g):
            copy.wait()
        start(across(g))
    pass_on(0)
    pass_up(1)
    rows_send(1)
    for g in range(1, GROUPS):
        start(to_mate(g))
        start(mate_qs(g))
    rest_near(0)

    q_row = lax.broadcasted_iota(jnp.int32, (TOK, 128), 0)
    k_lane = lax.broadcasted_iota(jnp.int32, (TOK, 128), 1)
    columns = []
    for j in range(2):
        mine = win[7 + j, pl.ds(0, 16), :].astype(jnp.float32)
        columns.append(jnp.sum(
            jnp.where(q_row == k_lane, mine[0:1], 0.0) + jnp.where(q_row == k_lane + 128, mine[1:2], 0.0),
            axis=1, keepdims=True))

    def mask(pairs):
        for j, pair in pairs:
            a, b = (win[j + 2 * pair + i, pl.ds(0, 16), :].astype(jnp.float32) for i in range(2))
            begin = (c - k - 7 + j) * TOK
            for i, keys_seg in enumerate((a[0:1], a[1:2] + b[2:3], b[3:4])):
                m = 3 * pair + i
                seen = (columns[j] == keys_seg) & (k_lane + 128 * m <= q_row + 7 * TOK) & (k_lane + 128 * m + begin >= 0)
                bias[j, :, 128 * m:128 * (m + 1)] = jnp.where(seen, 0.0, MASKED)

    mask(((0, 2), (0, 3), (1, 1), (1, 2), (1, 3)))
    rest_far(0)
    mask(((0, 0), (0, 1), (1, 0)))
    rest_far(GROUPS)

    def out_copy(j, g, part, sem):
        cols = pl.ds(pl.multiple_of((4 * k + g) * REPEAT * HD + part * WIDE, WIDE), WIDE)
        return pltpu.make_async_remote_copy(
            src_ref=ov.at[j, g, part], dst_ref=out_ref.at[0, :, cols],
            send_sem=out_send.at[sem], recv_sem=out_recv.at[(k * GROUPS + g) * PARTS + part],
            device_id=(1 - s, c - k + j), device_id_type=MESH)

    def step(t, _):
        g = t // (2 * PIECES)
        j = lax.rem(t // PIECES, 2)
        piece = lax.rem(t, PIECES)
        for i in range(1, GROUPS):
            @pl.when(t == 2 * PIECES * i)
            def _():
                rest_near(i)
                rest_far(i)

            @pl.when(t == 2 * PIECES * (i - 1) + 1)
            def _():
                pass_on(i)
                if i + 1 < GROUPS:
                    pass_up(i + 1)
                    rows_send(i + 1)

        cols = pl.ds(pl.multiple_of(piece * HEADS * HD, HEADS * HD), HEADS * HD)
        at_row = pl.multiple_of(SEG_ROWS + 2 * TOK * g, 16)
        key_rows = win[pl.ds(j, 8), pl.ds(at_row, TOK), :].reshape(8 * TOK, HD)
        value_rows = win[pl.ds(j, 8), pl.ds(pl.multiple_of(at_row + TOK, 16), TOK), :].reshape(8 * TOK, HD)
        q_all = qv[j, g, :, cols]
        before = sv[j, g, :, cols].astype(jnp.float32)

        def score_of(i):
            score = lax.dot_general(
                q_all[:, i * HD:(i + 1) * HD], key_rows, (((1,), (1,)), ((), ())), preferred_element_type=jnp.float32)
            return score + bias[j]

        score = score_of(0)
        for i in range(HEADS):
            later = score_of(i + 1) if i + 1 < HEADS else None
            top = jnp.max(score, axis=-1, keepdims=True)
            expo = jnp.exp2((score - top) * SCALE)
            total = jnp.sum(expo, axis=-1, keepdims=True)
            result = jnp.dot(expo.astype(jnp.bfloat16), value_rows, preferred_element_type=jnp.float32) / total
            part = 2 * piece + i // 2
            half = (i % 2) * HD
            ov[j, g, part, :, half:half + HD] = (before[:, i * HD:(i + 1) * HD] + result).astype(jnp.bfloat16)
            if i % 2:
                out_copy(j, g, part, 2 * t + i // 2).start()
            score = later
        return 0

    lax.fori_loop(0, 2 * GROUPS * PIECES, step, 0)

    def sent(copies):
        for copy in copies:
            copy.wait_send()

    for g in range(GROUPS):
        sent(mate_qs(g))
        for n in CHUNKS[g]:
            sent(to_mate(n))
            if g:
                sent(across(n))
            else:
                @pl.when((h == 0) | next1)
                def _():
                    sent(across(n))

            @pl.when(next1)
            def _():
                sent(to_next1(n))
                if g:
                    @pl.when(h == 0)
                    def _():
                        sent(lift(n))

                @pl.when(left)
                def _():
                    sent(forward(n))

            @pl.when(next1 & past1)
            def _():
                sent(far(n))

    def finish(t, _):
        out_copy(0, 0, 0, t).wait_send()
        pltpu.make_async_remote_copy(
            src_ref=ov.at[0, 0, 0], dst_ref=out_ref.at[0, :, pl.ds(0, WIDE)],
            send_sem=out_send.at[t], recv_sem=out_recv.at[t], device_id=mate, device_id_type=MESH).wait_recv()
        return 0

    lax.fori_loop(0, 2 * GROUPS * PARTS, finish, 0)


def solution(mesh):
    ctx = mesh.shape["ctx"]
    hbm = pl.BlockSpec(memory_space=pltpu.HBM)

    def local(stream, queries, keys, values, segments):
        copies = 2 * GROUPS * PARTS
        return pl.pallas_call(
            functools.partial(kernel, ctx),
            out_shape=jax.ShapeDtypeStruct(stream.shape, stream.dtype),
            in_specs=[hbm] * 5,
            out_specs=pl.BlockSpec(memory_space=pltpu.VMEM),
            scratch_shapes=[
                pltpu.VMEM((SLOTS, SEG_ROWS + 2 * TOK * GROUPS, HD), jnp.bfloat16),
                pltpu.VMEM((SEG_ROWS + 2 * TOK * GROUPS, HD), jnp.bfloat16),
                pltpu.VMEM((2, GROUPS, TOK, REPEAT * HD), jnp.bfloat16),
                pltpu.VMEM((2, GROUPS, TOK, REPEAT * HD), jnp.bfloat16),
                pltpu.VMEM((2, GROUPS, PARTS, TOK, WIDE), jnp.bfloat16),
                pltpu.VMEM((2, TOK, 8 * TOK), jnp.float32),
                pltpu.SemaphoreType.DMA((6, GROUPS)),
                pltpu.SemaphoreType.DMA((11, GROUPS + 1)),
                pltpu.SemaphoreType.DMA((SLOTS, GROUPS + 1)),
                pltpu.SemaphoreType.DMA((2, GROUPS)),
                pltpu.SemaphoreType.DMA((2, GROUPS)),
                pltpu.SemaphoreType.DMA((copies,)),
                pltpu.SemaphoreType.DMA((copies,)),
                pltpu.VMEM((1, TOK), jnp.int32),
                pltpu.SemaphoreType.DMA,
            ],
            compiler_params=pltpu.CompilerParams(
                collective_id=0, has_side_effects=True, vmem_limit_bytes=40 << 20),
        )(*[pltpu.with_memory_space_constraint(a, pltpu.HBM) for a in (stream, queries, keys, values, segments)])

    spec = P("section", "ctx", None)
    return jax.shard_map(
        local, mesh=mesh, in_specs=(spec, spec, spec, spec, P("section", "ctx")), out_specs=spec, check_vma=False)
```

```python
import functools

import jax
import jax.numpy as jnp
from jax import lax
from jax.experimental import pallas as pl
from jax.experimental.pallas import tpu as pltpu
from jax.sharding import PartitionSpec as P

MESH = pl.DeviceIdType.MESH
HD = 128
REPEAT = 8
TOK = 192
GROUPS = 4
PIECES = 2
HEADS = REPEAT // PIECES
PARTS = REPEAT // 2
WIDE = 2 * HD
SEG_ROWS = 16
CHUNKS = ((5, 0, 4), (1,), (2,), (3,))
SLOTS = 11
SCALE = HD ** -0.5 * 1.4426950408889634
MASKED = -1e30


def rows_of(chunk):
    if chunk == GROUPS + 1:
        return pl.ds(0, SEG_ROWS)
    if chunk == 0:
        return pl.ds(SEG_ROWS, TOK)
    if chunk == GROUPS:
        return pl.ds(SEG_ROWS + TOK, TOK)
    return pl.ds(SEG_ROWS + 2 * TOK * chunk, 2 * TOK)


def kernel(ctx, stream_ref, query_ref, key_ref, value_ref, seg_ref, out_ref,
           win, other, qv, sv, ov, bias, loc_sem, kv_send, kv_recv, qs_send, qs_recv, out_send, out_recv, seg_own, seg_sem):
    s = lax.axis_index("section")
    c = lax.axis_index("ctx")
    k = lax.rem(c, 2)
    h = lax.rem(c // 2, 2)
    line = c // 4
    lines = ctx // 4
    cross = 1 - 2 * k
    x_off = 2 - 4 * h
    next1 = line + 1 < lines
    past1, past2 = line >= 1, line >= 2
    left = (h == 1) | past1
    left3 = jnp.where(h == 1, past1, past2)
    mate = (s, c + cross)

    def at(offset):
        return (s, lax.rem(c + offset + ctx, ctx))

    def tell(sem, device):
        pl.semaphore_signal(sem, inc=1, device_id=device, device_id_type=MESH)

    barrier = pltpu.get_barrier_semaphore()
    for device in (mate, at(x_off), at(x_off + cross), (1 - s, c), (1 - s, c + cross)):
        tell(barrier, device)

    for there, offsets in (
        (next1, (4, 4 + cross)), (past1, (-4, -4 + cross)),
        (next1 & (h == 1), (2, 2 + cross)), (past1 & (h == 0), (-2, -2 + cross)),
    ):
        @pl.when(there)
        def _():
            for offset in offsets:
                tell(barrier, at(offset))

    def local_kv(g):
        out = []
        for half, (buf, base) in enumerate(((win.at[7 + k], 4 * k), (other, 4 - 4 * k))):
            cols = pl.ds(pl.multiple_of((base + g) * HD, HD), HD)
            for i, ref in enumerate((key_ref, value_ref)):
                rows = pl.ds(SEG_ROWS + 2 * TOK * g + TOK * i, TOK)
                out.append(pltpu.make_async_copy(ref.at[0, :, cols], buf.at[rows], loc_sem.at[2 * half + i, g]))
        return out

    def local_qs(g):
        cols = pl.ds(pl.multiple_of((4 * k + g) * REPEAT * HD, REPEAT * HD), REPEAT * HD)
        return [
            pltpu.make_async_copy(query_ref.at[0, :, cols], qv.at[k, g], loc_sem.at[4, g]),
            pltpu.make_async_copy(stream_ref.at[0, :, cols], sv.at[k, g], loc_sem.at[5, g]),
        ]

    def mate_qs(g):
        cols = pl.ds(pl.multiple_of((4 - 4 * k + g) * REPEAT * HD, REPEAT * HD), REPEAT * HD)
        return [
            pltpu.make_async_remote_copy(
                src_ref=ref.at[0, :, cols], dst_ref=buf.at[k, g], send_sem=qs_send.at[i, g], recv_sem=qs_recv.at[i, g],
                device_id=mate, device_id_type=MESH)
            for i, (ref, buf) in enumerate(((query_ref, qv), (stream_ref, sv)))
        ]

    def kv_copy(src, slot, g, device, sem):
        return pltpu.make_async_remote_copy(
            src_ref=src.at[rows_of(g)], dst_ref=win.at[slot].at[rows_of(g)],
            send_sem=kv_send.at[sem, g], recv_sem=kv_recv.at[slot, g], device_id=device, device_id_type=MESH)

    def arrived(slot, g):
        kv_copy(win.at[slot], slot, g, mate, 0).wait_recv()

    own = win.at[7 + k]

    def to_mate(g):
        return [kv_copy(other, 7 + k, g, mate, 0)]

    def to_next1(g):
        return [kv_copy(own, 3 + k, g, at(4), 1), kv_copy(other, 3 + k, g, at(4 + cross), 2)]

    def far(n):
        return [kv_copy(win.at[4], 0, n, at(4), 3)]

    def across(g):
        slot = 5 + 4 * h + k
        return [kv_copy(own, slot, g, at(x_off), 5), kv_copy(other, slot, g, at(x_off + cross), 6)]

    def to_next_first(n):
        return [kv_copy(own, 5 + k, n, at(2), 5), kv_copy(other, 5 + k, n, at(2 + cross), 6)]

    def lift(g):
        return [kv_copy(win.at[9 + i], 5 + i, g, at(4), 9 + i) for i in range(2)]

    def forward(g):
        return [kv_copy(win.at[5 + i], 1 + i, g, at(4), 7 + i) for i in range(2)]

    def start(copies):
        for copy in copies:
            copy.start()

    def rows_send(g):
        @pl.when(next1)
        def _():
            for n in CHUNKS[g]:
                start(to_next1(n))

    def pass_up(g):
        @pl.when(h == 0)
        def _():
            arrived(9, g)
            arrived(10, g)

            @pl.when(next1)
            def _():
                start(lift(g))

    def pass_on(g):
        @pl.when(past1)
        def _():
            for n in CHUNKS[g]:
                arrived(4, n)

                @pl.when(next1)
                def _():
                    start(far(n))

        @pl.when(left)
        def _():
            for n in CHUNKS[g]:
                for i in range(2):
                    arrived(5 + i, n)

                    @pl.when(next1)
                    def _():
                        start(forward(n)[i:i + 1])

    def rest_near(g):
        for n in CHUNKS[g]:
            @pl.when(past1)
            def _():
                arrived(3, n)
            arrived(8 - k, n)
        for copy in local_qs(g):
            copy.wait()
        for copy in mate_qs(g):
            copy.wait_recv()

    def rest_far(n):
        @pl.when(left3)
        def _():
            arrived(1, n)
            arrived(2, n)

        @pl.when(past2)
        def _():
            arrived(0, n)

    seg_copy = pltpu.make_async_copy(seg_ref, seg_own, seg_sem)
    seg_copy.start()
    for g in range(GROUPS):
        start(local_kv(g))
        start(local_qs(g))
    seg_copy.wait()

    lane = lax.broadcasted_iota(jnp.int32, (16, 128), 1)
    row = lax.broadcasted_iota(jnp.int32, (16, 128), 0)
    seg = seg_own[...].astype(jnp.float32)
    first = jnp.broadcast_to(seg[:, :128], (16, 128))
    last = jnp.broadcast_to(jnp.concatenate([seg[:, 128:], jnp.zeros((1, 64), jnp.float32)], axis=1), (16, 128))
    first_moved = pltpu.roll(first, 64, 1)
    last_moved = pltpu.roll(last, 64, 1)
    tile = jnp.where(row == 0, first, jnp.where(row == 1, last, jnp.where(
        row == 2, jnp.where(lane >= 64, first_moved, 0.0), jnp.where(lane < 64, first_moved, last_moved))))
    tile = tile.astype(jnp.bfloat16)
    win[7 + k, pl.ds(0, 16), :] = tile
    other[pl.ds(0, 16), :] = tile

    def clear(slot, _):
        win[slot] = jnp.zeros(win.shape[1:], win.dtype)
        return 0

    lax.fori_loop(0, jnp.maximum(7 - 2 * (c // 2), 0), clear, 0)

    def count(flag, times):
        return times * flag.astype(jnp.int32)

    pl.semaphore_wait(barrier, 5 + count(next1, 2) + count(past1, 2)
                      + count(next1 & (h == 1), 2) + count(past1 & (h == 0), 2))

    for copy in local_kv(0):
        copy.wait()

    for n in CHUNKS[0]:
        @pl.when(h == 0)
        def _():
            start(across(n))

        @pl.when(next1 & (h == 1))
        def _():
            start(to_next_first(n))
    for n in CHUNKS[0]:
        start(to_mate(n))
    start(mate_qs(0))
    rows_send(0)

    for g in range(1, GROUPS):
        for copy in local_kv(g):
            copy.wait()
        start(across(g))
    pass_on(0)
    pass_up(1)
    rows_send(1)
    for g in range(1, GROUPS):
        start(to_mate(g))
        start(mate_qs(g))
    rest_near(0)

    q_row = lax.broadcasted_iota(jnp.int32, (TOK, 128), 0)
    k_lane = lax.broadcasted_iota(jnp.int32, (TOK, 128), 1)
    columns = []
    for j in range(2):
        mine = win[7 + j, pl.ds(0, 16), :].astype(jnp.float32)
        columns.append(jnp.sum(
            jnp.where(q_row == k_lane, mine[0:1], 0.0) + jnp.where(q_row == k_lane + 128, mine[1:2], 0.0),
            axis=1, keepdims=True))

    def mask(pairs):
        for j, pair in pairs:
            a, b = (win[j + 2 * pair + i, pl.ds(0, 16), :].astype(jnp.float32) for i in range(2))
            begin = (c - k - 7 + j) * TOK
            for i, keys_seg in enumerate((a[0:1], a[1:2] + b[2:3], b[3:4])):
                m = 3 * pair + i
                seen = (columns[j] == keys_seg) & (k_lane + 128 * m <= q_row + 7 * TOK) & (k_lane + 128 * m + begin >= 0)
                bias[j, :, 128 * m:128 * (m + 1)] = jnp.where(seen, 0.0, MASKED)

    mask(((0, 2), (0, 3), (1, 1), (1, 2), (1, 3)))
    rest_far(GROUPS + 1)
    mask(((0, 0), (0, 1), (1, 0)))
    rest_far(0)
    rest_far(GROUPS)

    def out_copy(j, g, part, sem):
        cols = pl.ds(pl.multiple_of((4 * k + g) * REPEAT * HD + part * WIDE, WIDE), WIDE)
        return pltpu.make_async_remote_copy(
            src_ref=ov.at[j, g, part], dst_ref=out_ref.at[0, :, cols],
            send_sem=out_send.at[sem], recv_sem=out_recv.at[(k * GROUPS + g) * PARTS + part],
            device_id=(1 - s, c - k + j), device_id_type=MESH)

    def step(t, _):
        g = t // (2 * PIECES)
        j = lax.rem(t // PIECES, 2)
        piece = lax.rem(t, PIECES)
        for i in range(1, GROUPS):
            @pl.when(t == 2 * PIECES * i)
            def _():
                rest_near(i)
                rest_far(i)

            @pl.when(t == 2 * PIECES * (i - 1) + 1)
            def _():
                pass_on(i)
                if i + 1 < GROUPS:
                    pass_up(i + 1)
                    rows_send(i + 1)

        cols = pl.ds(pl.multiple_of(piece * HEADS * HD, HEADS * HD), HEADS * HD)
        at_row = pl.multiple_of(SEG_ROWS + 2 * TOK * g, 16)
        key_rows = win[pl.ds(j, 8), pl.ds(at_row, TOK), :].reshape(8 * TOK, HD)
        value_rows = win[pl.ds(j, 8), pl.ds(pl.multiple_of(at_row + TOK, 16), TOK), :].reshape(8 * TOK, HD)
        q_all = qv[j, g, :, cols]
        before = sv[j, g, :, cols].astype(jnp.float32)

        def score_of(i):
            score = lax.dot_general(
                q_all[:, i * HD:(i + 1) * HD], key_rows, (((1,), (1,)), ((), ())), preferred_element_type=jnp.float32)
            return score + bias[j]

        score = score_of(0)
        for i in range(HEADS):
            later = score_of(i + 1) if i + 1 < HEADS else None
            top = jnp.max(score, axis=-1, keepdims=True)
            expo = jnp.exp2((score - top) * SCALE)
            total = jnp.sum(expo, axis=-1, keepdims=True)
            result = jnp.dot(expo.astype(jnp.bfloat16), value_rows, preferred_element_type=jnp.float32) / total
            part = 2 * piece + i // 2
            half = (i % 2) * HD
            ov[j, g, part, :, half:half + HD] = (before[:, i * HD:(i + 1) * HD] + result).astype(jnp.bfloat16)
            if i % 2:
                out_copy(j, g, part, 2 * t + i // 2).start()
            score = later
        return 0

    lax.fori_loop(0, 2 * GROUPS * PIECES, step, 0)

    def sent(copies):
        for copy in copies:
            copy.wait_send()

    for g in range(GROUPS):
        sent(mate_qs(g))
        for n in CHUNKS[g]:
            sent(to_mate(n))
            if g:
                sent(across(n))
            else:
                @pl.when((h == 0) | next1)
                def _():
                    sent(across(n))

            @pl.when(next1)
            def _():
                sent(to_next1(n))
                if g:
                    @pl.when(h == 0)
                    def _():
                        sent(lift(n))

                @pl.when(left)
                def _():
                    sent(forward(n))

            @pl.when(next1 & past1)
            def _():
                sent(far(n))

    def finish(t, _):
        out_copy(0, 0, 0, t).wait_send()
        pltpu.make_async_remote_copy(
            src_ref=ov.at[0, 0, 0], dst_ref=out_ref.at[0, :, pl.ds(0, WIDE)],
            send_sem=out_send.at[t], recv_sem=out_recv.at[t], device_id=mate, device_id_type=MESH).wait_recv()
        return 0

    lax.fori_loop(0, 2 * GROUPS * PARTS, finish, 0)


def solution(mesh):
    ctx = mesh.shape["ctx"]
    hbm = pl.BlockSpec(memory_space=pltpu.HBM)

    def local(stream, queries, keys, values, segments):
        copies = 2 * GROUPS * PARTS
        return pl.pallas_call(
            functools.partial(kernel, ctx),
            out_shape=jax.ShapeDtypeStruct(stream.shape, stream.dtype),
            in_specs=[hbm] * 5,
            out_specs=pl.BlockSpec(memory_space=pltpu.VMEM),
            scratch_shapes=[
                pltpu.VMEM((SLOTS, SEG_ROWS + 2 * TOK * GROUPS, HD), jnp.bfloat16),
                pltpu.VMEM((SEG_ROWS + 2 * TOK * GROUPS, HD), jnp.bfloat16),
                pltpu.VMEM((2, GROUPS, TOK, REPEAT * HD), jnp.bfloat16),
                pltpu.VMEM((2, GROUPS, TOK, REPEAT * HD), jnp.bfloat16),
                pltpu.VMEM((2, GROUPS, PARTS, TOK, WIDE), jnp.bfloat16),
                pltpu.VMEM((2, TOK, 8 * TOK), jnp.float32),
                pltpu.SemaphoreType.DMA((6, GROUPS)),
                pltpu.SemaphoreType.DMA((11, GROUPS + 2)),
                pltpu.SemaphoreType.DMA((SLOTS, GROUPS + 2)),
                pltpu.SemaphoreType.DMA((2, GROUPS)),
                pltpu.SemaphoreType.DMA((2, GROUPS)),
                pltpu.SemaphoreType.DMA((copies,)),
                pltpu.SemaphoreType.DMA((copies,)),
                pltpu.VMEM((1, TOK), jnp.int32),
                pltpu.SemaphoreType.DMA,
            ],
            compiler_params=pltpu.CompilerParams(
                collective_id=0, has_side_effects=True, vmem_limit_bytes=40 << 20),
        )(*[pltpu.with_memory_space_constraint(a, pltpu.HBM) for a in (stream, queries, keys, values, segments)])

    spec = P("section", "ctx", None)
    return jax.shard_map(
        local, mesh=mesh, in_specs=(spec, spec, spec, spec, P("section", "ctx")), out_specs=spec, check_vma=False)
```
